32 devices in a mesh: gx: 8 (over y, x, core), gz: 4 (over z).
Axes of the slice: x: 2, y: 2, z: 4, core: 2. Of those that a mesh axis runs over, the one named last changes fastest.
Arguments:
- pressure_now: float32 [128, 128, 512], P('gz', 'gx'), may hold values from -6 to 6
- pressure_prev: float32 [128, 128, 512], P('gz', 'gx'), may hold values from -6 to 6
- adjoint_now: float32 [128, 128, 512], P('gz', 'gx'), may hold values from -6 to 6
- adjoint_prev: float32 [128, 128, 512], P('gz', 'gx'), may hold values from -6 to 6
- speed2: float32 [128, 128, 512], P('gz', 'gx'), may hold values from 0.05 to 0.32
- layer_state: float32 [4096, 64, 128], P(('gx', 'gz')), may hold values from -3 to 3
- layer_maps: float32 [8, 64, 64], replicated, as said below
- send_rows: int32 [32, 32, 4], P(('gx', 'gz')), may hold values from -1 to 2047, as said below
- slot_patch: int32 [4096], P(('gx', 'gz')), may hold values from 0 to 255
- patch_material: int32 [256], replicated, may hold values from 0 to 7
Outputs:
- pressure_out: float32 [128, 128, 512], P('gz', 'gx')
- adjoint_out: float32 [128, 128, 512], P('gz', 'gx')
- patch_gradient: float32 [256, 128], P(('gx', 'gz'))
The draws below stay inside these ranges and needn't reach their ends.
Inputs may be any that keep to these rules, and one draw needn't show every extreme that they name: `send_rows`: each device's non-negative entries are distinct rows of its tile; -1 marks an unused entry; for one device every entry aimed at it is used. `layer_maps`: each material's matrix has diagonal entries from 0.5 to 0.9.
All inputs are finite; a program needn't handle non-finite values.
Results may differ from the reference program's by a relative error of at most 0.00016.
Values sent between devices are 32-bit elements; how exact they have to be, the bound alone decides.
A program may use at most 192 MiB of HBM per device.

```python
import math
import jax
import jax.numpy as jnp
import numpy as np
from jax import lax

CX = 16
CZ = 32
NY = 512
W = 128
DEPTH = 64
SLOT_DEV = 128
MATS = 8
STEPS = 4
NX = 128
NZ = 128
ROWS_TILE = 2048
CAP = 4
PATCHES = 256
N_GX = 8
N_GZ = 4
DEVICES = 32


def draw_layer_maps(key, part):
    first, second = jax.random.split(key)
    diag = jax.random.uniform(first, (MATS, DEPTH), jnp.float32, 0.5, 0.9)
    spread = 0.4 / math.sqrt(DEPTH)
    off = jax.random.normal(second, (MATS, DEPTH, DEPTH), jnp.float32) * spread
    ident = jnp.eye(DEPTH, dtype=jnp.float32)
    return ident[None, :, :] * diag[:, :, None] + off * (1.0 - ident[None, :, :])


def draw_send_rows(key, part):
    key_fill, key_full, key_coin, key_perm = jax.random.split(key, 4)
    fill = jax.random.randint(key_fill, (DEVICES,), 300, 1001)
    fullest = jax.random.randint(key_full, (), 0, DEVICES)
    fill = jnp.where(jnp.arange(DEVICES) == fullest, 1001, fill)
    coin = jax.random.randint(key_coin, (DEVICES, DEVICES, CAP), 0, 1000)
    live = coin < fill[None, :, None]
    keys = jax.random.split(key_perm, DEVICES)
    picks = jax.vmap(lambda single: jax.random.permutation(single, ROWS_TILE)[:SLOT_DEV])(keys)
    picks = picks.reshape(DEVICES, DEVICES, CAP).astype(jnp.int32)
    return jnp.where(live, picks, -1).astype(jnp.int32)


def set_ends(result, stream_key, low, top_value):
    spot = [jax.random.randint(jax.random.fold_in(stream_key, axis), (), 0, length) for axis, length in enumerate(result.shape)]
    widest = result.shape.index(max(result.shape))
    neighbour = spot[:widest] + [(spot[widest] + 1) % result.shape[widest]] + spot[widest + 1:]
    return result.at[tuple(spot)].set(low).at[tuple(neighbour)].set(top_value)


def block_levels(rng, dims, cuts, smallest, top_value):
    loudness = 1.0
    for dim, parts in cuts:
        draws = jax.random.uniform(jax.random.fold_in(jax.random.fold_in(rng, 6), dim), (parts,), jnp.float32, smallest / len(cuts), top_value / len(cuts))
        loudness = loudness * jnp.repeat(jnp.exp(draws), dims[dim] // parts).reshape((-1,) + (1,) * (len(dims) - 1 - dim))
    return loudness


def rank_bounds(amount, lean):
    loads = [(1 << 20) // math.isqrt(grade ** lean) + 1 for grade in range(1, amount + 1)]
    width = 1 + sum(loads) // (1 << 30)
    return np.cumsum(np.array([max(1, weight // width) for weight in loads]))


def skewed_ids(key, extent, count, skew):
    grid = rank_bounds(count, skew)
    lot = jax.random.randint(jax.random.fold_in(key, 1), extent, 0, int(grid[count - 1]))
    rank = jnp.searchsorted(jnp.asarray(grid, jnp.int32), lot, side="right")
    return jax.random.permutation(jax.random.fold_in(key, 2), count)[rank].astype(jnp.int32)


def normal_values(rng, dims, deviation, reach, cuts=(), kind=jnp.bfloat16):
    entries = jax.random.normal(rng, dims, jnp.float32) * deviation
    if len(cuts) > 0:
        entries = block_levels(rng, dims, cuts, -0.22, 0.18) * entries
    return jnp.clip(entries, min=-reach, max=reach).astype(kind)


def setup_inputs(seed: int = 0) -> dict:
    seeds = jax.random.split(jax.random.key(seed), 11)
    pressure_now = normal_values(seeds[0], (NZ, NX, NY), 1.0, 6.0, ((0, 4), (1, 8)), jnp.float32)
    pressure_prev = normal_values(seeds[1], (NZ, NX, NY), 1.0, 6.0, ((0, 4), (1, 8)), jnp.float32)
    adjoint_now = normal_values(seeds[2], (NZ, NX, NY), 1.0, 6.0, ((0, 4), (1, 8)), jnp.float32)
    adjoint_prev = normal_values(seeds[3], (NZ, NX, NY), 1.0, 6.0, ((0, 4), (1, 8)), jnp.float32)
    speed2 = jnp.clip(jnp.exp(math.log(0.32) - 1.856298 * jax.random.uniform(seeds[4], (NZ, NX, NY), jnp.float32) ** block_levels(seeds[4], (NZ, NX, NY), ((0, 4), (1, 8)), -0.2, 0.2)), 0.05, 0.32)
    layer_state = normal_values(seeds[5], (DEVICES * SLOT_DEV, DEPTH, W), 0.5, 3.0, ((0, 32),), jnp.float32)
    layer_maps = draw_layer_maps(jax.random.fold_in(seeds[10], 71), 0)
    send_rows = draw_send_rows(jax.random.fold_in(seeds[10], 71), 0)
    slot_patch = set_ends(skewed_ids(seeds[8], (DEVICES * SLOT_DEV,), PATCHES, 2), jax.random.fold_in(seeds[8], 3), 0, PATCHES - 1).astype(jnp.int32)
    patch_material = set_ends(jax.random.randint(seeds[9], (PATCHES,), 0, MATS), jax.random.fold_in(seeds[9], 1), 0, MATS - 1).astype(jnp.int32)
    return dict(pressure_now=pressure_now, pressure_prev=pressure_prev, adjoint_now=adjoint_now, adjoint_prev=adjoint_prev, speed2=speed2, layer_state=layer_state, layer_maps=layer_maps, send_rows=send_rows, slot_patch=slot_patch, patch_material=patch_material)


KAPPA = 0.5
BETA = 0.3


def to_rows(field):
    blocks = field.reshape(N_GZ, CZ, N_GX, CX, NY // W, W).transpose(2, 0, 1, 3, 4, 5)
    return blocks.reshape(N_GX * N_GZ, CZ * CX * (NY // W), W)


def from_rows(rows):
    blocks = rows.reshape(N_GX, N_GZ, CZ, CX, NY // W, W).transpose(1, 2, 0, 3, 4, 5)
    return blocks.reshape(N_GZ * CZ, N_GX * CX, NY)


def laplace(field):
    padded = jnp.pad(field, 1)
    beside = padded[2:, 1:-1, 1:-1] + padded[:-2, 1:-1, 1:-1]
    beside = beside + padded[1:-1, 2:, 1:-1] + padded[1:-1, :-2, 1:-1]
    beside = beside + padded[1:-1, 1:-1, 2:] + padded[1:-1, 1:-1, :-2]
    return beside - 6.0 * field


def place_rows(target, delta):
    empty = jnp.zeros((ROWS_TILE, W), jnp.float32)
    return empty.at[target].add(delta, mode="drop")


def relay_step(field, previous, speed2, layer, maps, send_rows):
    devices = N_GX * N_GZ
    rows = to_rows(field)
    sources = send_rows.reshape(devices, SLOT_DEV)
    valid = sources >= 0
    picked = jnp.take_along_axis(rows, jnp.maximum(sources, 0)[:, :, None], axis=1)
    picked = jnp.where(valid[:, :, None], picked, 0.0)
    air = picked.reshape(devices, devices, CAP, W).transpose(1, 0, 2, 3).reshape(devices * SLOT_DEV, W)
    push = KAPPA * (air - layer[:, 0, :])
    fresh = jnp.einsum("sij,sjw->siw", maps, layer, precision=lax.Precision.HIGHEST)
    fresh = fresh + maps[:, :, 0][:, :, None] * push[:, None, :]
    back = fresh[:, 0, :].reshape(devices, devices, CAP, W).transpose(1, 0, 2, 3).reshape(devices, SLOT_DEV, W)
    delta = jnp.where(valid[:, :, None], BETA * (back - picked), 0.0)
    target = jnp.where(valid, sources, ROWS_TILE).astype(jnp.int32)
    coupling = jax.vmap(place_rows)(target, delta)
    following = 2.0 * field - previous + speed2 * laplace(field) + from_rows(coupling)
    return following, fresh


def reference(pressure_now, pressure_prev, adjoint_now, adjoint_prev, speed2, layer_state, layer_maps, send_rows, slot_patch, patch_material):
    materials = jnp.take(patch_material, slot_patch)
    forward_maps = jnp.take(layer_maps, materials, axis=0)
    adjoint_maps = jnp.swapaxes(forward_maps, 1, 2)
    layer_f = layer_state
    layer_a = jnp.zeros_like(layer_state)
    forward_layers = []
    adjoint_layers = []
    for step in range(STEPS):
        following, layer_f = relay_step(pressure_now, pressure_prev, speed2, layer_f, forward_maps, send_rows)
        pressure_prev, pressure_now = pressure_now, following
        following, layer_a = relay_step(adjoint_now, adjoint_prev, speed2, layer_a, adjoint_maps, send_rows)
        adjoint_prev, adjoint_now = adjoint_now, following
        forward_layers.append(layer_f)
        adjoint_layers.append(layer_a)
    correlation = jnp.zeros((layer_state.shape[0], W), jnp.float32)
    for step in range(STEPS):
        correlation = correlation + jnp.sum(forward_layers[step] * adjoint_layers[STEPS - 1 - step], axis=1)
    patch_gradient = jax.ops.segment_sum(correlation, slot_patch, num_segments=PATCHES)
    return pressure_now, adjoint_now, patch_gradient
```

```python
import functools

import jax
import jax.numpy as jnp
from jax import lax
from jax.experimental import pallas as pl
from jax.experimental.pallas import tpu as pltpu
from jax.sharding import PartitionSpec as P

STEPS = 4
KAPPA = 0.5
BETA = 0.3
TERMS = STEPS + 1
LANES = 128
CHUNK = 16
ORDER = (("a", 0), ("a", 1), ("p", 0), ("a", 2), ("p", 1), ("a", 3), ("p", 2), ("p", 3))
F32 = jnp.float32
BF16 = jnp.bfloat16
MESH = pl.DeviceIdType.MESH


def split(value):
    high = value.astype(BF16)
    return high, (value - high.astype(F32)).astype(BF16)


def kernel_body(
    nx, nz,
    patch_s, material_s, rows_s, maps, src_lane, src_column,
    p_now_h, p_prev_h, a_now_h, a_prev_h, speed2_h, state_h,
    p_out, a_out, grad_out,
    p_now, p_prev, p_mid, a_now, a_prev, a_mid, speed2, state,
    spread, couple, hist, weights, chain, table, ctab,
    info_send, info_recv, info, relay_send, relay_recv, surf, backs, scale,
    grad_send, grad_recv, x_send, x_recv, z_recv,
    load_sem, chunk_sem, send_sem, recv_sem,
    info_ssem, info_rsem, relay_ssem, relay_rsem, grad_ssem, grad_rsem,
):
    cz, blocks, cx, _ = speed2.shape
    slots = src_lane.shape[1]
    devices = nx * nz
    cap = slots // devices
    mats, depth, _ = maps.shape
    patches = material_s.shape[0]
    own = patches // devices
    chunks = slots // CHUNK
    peers = CHUNK // cap

    gx, gz = lax.axis_index("gx"), lax.axis_index("gz")
    me = gx * nz + gz
    exists = [gx > 0, gx < nx - 1, gz > 0, gz < nz - 1]
    target = [(gx - 1, gz), (gx + 1, gz), (gx, gz - 1), (gx, gz + 1)]

    def where_is(flat):
        return (lax.div(flat, nz), lax.rem(flat, nz))

    first_chunk = lax.div(me * cap, CHUNK)
    loads = {}
    for i, (name, src, dst) in enumerate((
        ("a", a_now_h, a_now), ("p", p_now_h, p_now),
        ("ap", a_prev_h, a_prev), ("s", speed2_h, speed2), ("pp", p_prev_h, p_prev),
    )):
        loads[name] = [
            pltpu.make_async_copy(
                src.at[:, :, pl.ds(rb * LANES, LANES)], dst.at[:, rb], load_sem.at[i, rb]
            )
            for rb in range(blocks)
        ]

    def chunk_copy(j):
        at = lax.rem(first_chunk + j, chunks) * CHUNK
        return pltpu.make_async_copy(
            state_h.at[pl.ds(at, CHUNK)], state.at[pl.ds(at, CHUNK)], chunk_sem.at[j]
        )

    barrier = pltpu.get_barrier_semaphore()

    @pl.loop(1, devices)
    def _(o):
        pl.semaphore_signal(
            barrier, inc=1, device_id=where_is(lax.rem(me + o, devices)), device_id_type=MESH
        )

    for name in ("a", "p"):
        for copy in loads[name]:
            copy.start()

    @pl.loop(0, chunks)
    def _(j):
        chunk_copy(j).start()

    for name in ("ap", "s", "pp"):
        for copy in loads[name]:
            copy.start()

    row8 = lax.broadcasted_iota(jnp.int32, (mats, LANES), 0)
    lane8 = lax.broadcasted_iota(jnp.int32, (mats, LANES), 1)
    halve = jnp.where(lane8 % depth == 0, 1.0 - KAPPA, 1.0)
    for j in range(mats // 2):
        high, low = split(jnp.concatenate([maps[2 * j], maps[2 * j + 1]], axis=1))
        weights[:, j * LANES : (j + 1) * LANES] = jnp.concatenate([high, low, high, low], axis=0)
    v = jnp.concatenate([maps[m, 0:1, :] for m in range(mats)], axis=0)
    v = jnp.concatenate([v, v], axis=1) * halve
    coefs = jnp.zeros((mats, LANES), F32)
    for n in range(TERMS):
        chain[n] = v
        coefs = jnp.where(lane8 == n, v[:, 0:1] * (KAPPA / (1.0 - KAPPA)), coefs)
        if n < TERMS - 1:
            high, low = split(v)
            got = jnp.dot(
                jnp.concatenate([high, low], axis=1), weights[...], preferred_element_type=F32
            )
            total = jnp.zeros((mats, LANES), F32)
            for j in range(mats // 2):
                keep = 2 * j + lane8 // depth == row8
                total = total + jnp.where(keep, got[:, j * LANES : (j + 1) * LANES], 0.0)
            v = (total + pltpu.roll(total, depth, 1)) * halve
    ctab[...] = coefs
    low_half = lax.broadcasted_iota(jnp.int32, (8, LANES), 1) < depth
    for m in range(mats):
        rows = jnp.concatenate(
            [chain[n, m : m + 1, :] for n in range(TERMS)] + [jnp.zeros((8 - TERMS, LANES), F32)],
            axis=0,
        )
        high = rows.astype(BF16)
        low = jnp.where(low_half, rows - high.astype(F32), 0.0).astype(BF16)
        table[m] = jnp.concatenate([high, low], axis=0)

    lane1 = lax.broadcasted_iota(jnp.int32, (1, LANES), 1)

    @pl.loop(0, devices)
    def _(k):
        for c in range(cap):
            patch = patch_s[k * cap + c]
            coef = ctab[pl.ds(material_s[patch], 1), :]
            ids = jnp.full((1, LANES), patch, jnp.int32).astype(F32)
            info_send[k, c : c + 1, :] = jnp.where(lane1 == TERMS, ids, coef)

    now = {"p": p_now, "a": a_now}
    buffers = {"p": (p_prev, p_now, p_mid), "a": (a_prev, a_now, a_mid)}
    outs = {"p": p_out, "a": a_out}
    which = {"p": 0, "a": 1}

    def halo_copy(name, step, d, source):
        field = which[name]
        if d < 2:
            ref, dst = x_send.at[step, field, d], x_recv.at[step, field, 1 - d]
        else:
            ref = source.at[0 if d == 2 else cz - 1]
            dst = z_recv.at[step, field, 3 - d]
        return pltpu.make_async_remote_copy(
            src_ref=ref, dst_ref=dst,
            send_sem=send_sem.at[step, field, d],
            recv_sem=recv_sem.at[step, field, d ^ 1],
            device_id=target[d], device_id_type=MESH,
        )

    def start_halo(name, step, source):
        for d in range(4):
            @pl.when(exists[d])
            def _(d=d):
                halo_copy(name, step, d, source).start()

    def wait_recv(name, step):
        field = which[name]
        for d in range(4):
            @pl.when(exists[d])
            def _(d=d):
                side = x_recv.at[step, field, d] if d < 2 else z_recv.at[step, field, d - 2]
                pltpu.make_async_remote_copy(
                    src_ref=side, dst_ref=side,
                    send_sem=send_sem.at[step, field, d],
                    recv_sem=recv_sem.at[step, field, d],
                    device_id=target[d], device_id_type=MESH,
                ).wait_recv()

    def wait_send(name, step, source):
        for d in range(4):
            @pl.when(exists[d])
            def _(d=d):
                halo_copy(name, step, d, source).wait_send()

    for d in range(4):
        @pl.when(jnp.logical_not(exists[d]))
        def _(d=d):
            for step in range(STEPS):
                for field in range(2):
                    if d < 2:
                        x_recv[step, field, d] = jnp.zeros((cz, blocks, LANES), F32)
                    else:
                        z_recv[step, field, d - 2] = jnp.zeros((blocks, cx, LANES), F32)

    lanes = src_lane[...]
    xrow = lax.broadcasted_iota(jnp.int32, (cx, slots), 0)

    @pl.loop(0, cz)
    def _(z):
        for rb in range(blocks):
            row = z * (cx * blocks) + xrow * blocks + rb
            hit = jnp.where(row == lanes, 1.0, 0.0).astype(BF16)
            spread[z, rb] = jnp.concatenate([hit, hit], axis=1)

    for name in ("a", "p"):
        for copy in loads[name]:
            copy.wait()

        @pl.loop(0, cz)
        def _(z, name=name):
            for rb in range(blocks):
                x_send[0, which[name], 0, z, rb : rb + 1, :] = now[name][z, rb, 0:1, :]
                x_send[0, which[name], 1, z, rb : rb + 1, :] = now[name][z, rb, cx - 1 : cx, :]

    pl.semaphore_wait(barrier, devices - 1)
    start_halo("a", 0, now["a"])
    start_halo("p", 0, now["p"])

    @pl.loop(1, devices)
    def _(o):
        k = lax.rem(me + o, devices)
        pltpu.make_async_remote_copy(
            src_ref=info_send.at[k], dst_ref=info_recv.at[me],
            send_sem=info_ssem, recv_sem=info_rsem,
            device_id=where_is(k), device_id_type=MESH,
        ).start()

    def relay_copy(k, part):
        rows = pl.ds(0, 1) if part == 0 else pl.ds(1, TERMS - 1)
        return pltpu.make_async_remote_copy(
            src_ref=relay_send.at[k, rows], dst_ref=relay_recv.at[me, rows],
            send_sem=relay_ssem.at[part], recv_sem=relay_rsem.at[part],
            device_id=where_is(k), device_id_type=MESH,
        )

    @pl.loop(0, chunks)
    def _(j):
        chunk = lax.rem(first_chunk + j, chunks)
        chunk_copy(j).wait()
        for pair in range(CHUNK // 2):
            at = chunk * CHUNK + 2 * pair
            mat = [material_s[patch_s[at + i]] for i in range(2)]
            data = jnp.concatenate([state[at], state[at + 1]], axis=1)
            high, low = split(data)
            both = jnp.dot(
                jnp.concatenate([table[mat[0]], table[mat[1]]], axis=0),
                jnp.concatenate([high, low], axis=0), preferred_element_type=F32,
            )
            for i in range(2):
                part = both[16 * i : 16 * i + 16, i * LANES : (i + 1) * LANES]
                got = part[:8] + part[8:]
                slot = 2 * pair + i
                for n in range(TERMS):
                    relay_send[
                        chunk * peers + slot // cap, n, slot % cap : slot % cap + 1, :
                    ] = got[n : n + 1]
        for q in range(peers):
            k = chunk * peers + q
            @pl.when(k != me)
            def _(k=k):
                relay_copy(k, 0).start()
                relay_copy(k, 1).start()

    def gather(source, name, step):
        field = which[name]

        @pl.loop(0, slots // 8)
        def _(b):
            base = pl.multiple_of(b * 8, 8)
            picked = []
            for i in range(8):
                r = jnp.maximum(rows_s[base + i], 0)
                z = lax.div(r, cx * blocks)
                x = lax.rem(lax.div(r, blocks), cx)
                picked.append(source[z, lax.rem(r, blocks), pl.ds(x, 1), :])
            valid = src_column[pl.ds(base, 8), :] >= 0
            hist[field, step, pl.ds(base, 8), :] = jnp.where(
                valid, jnp.concatenate(picked, axis=0), 0.0
            )

    def wait_info():
        side = info_recv.at[pl.ds(0, devices - 1)]
        pltpu.make_async_remote_copy(
            src_ref=side, dst_ref=side, send_sem=info_ssem, recv_sem=info_rsem,
            device_id=where_is(lax.rem(me + 1, devices)), device_id_type=MESH,
        ).wait_recv()
        info_recv[me] = info_send[me]
        for k in range(devices):
            info[k * cap : (k + 1) * cap, :] = info_recv[k]
        for n in range(TERMS):
            scale[n] = jnp.broadcast_to(info[:, n : n + 1], (slots, LANES))

    def wait_relay(part):
        rows = pl.ds(0, 1) if part == 0 else pl.ds(1, TERMS - 1)
        side = relay_recv.at[pl.ds(0, devices - 1), rows]
        pltpu.make_async_remote_copy(
            src_ref=side, dst_ref=side, send_sem=relay_ssem.at[part], recv_sem=relay_rsem.at[part],
            device_id=where_is(lax.rem(me + 1, devices)), device_id_type=MESH,
        ).wait_recv()
        for n in ([0] if part == 0 else range(1, TERMS)):
            relay_recv[me, n] = relay_send[me, n]
            for k in range(devices):
                surf[n, k * cap : (k + 1) * cap, :] = relay_recv[k, n]

    def grad_copy(k):
        return pltpu.make_async_remote_copy(
            src_ref=grad_send.at[k], dst_ref=grad_recv.at[me],
            send_sem=grad_ssem, recv_sem=grad_rsem,
            device_id=where_is(k), device_id_type=MESH,
        )

    def correlate():
        total = jnp.zeros((slots, LANES), F32)
        for t in range(STEPS):
            inner = float(STEPS - t) * surf[STEPS - t]
            for q in range(STEPS - t):
                inner = inner + float(STEPS - t - q) * scale[STEPS - t - q] * hist[0, q]
                inner = inner + scale[STEPS - 1 - t - q] * backs[q]
            total = total + KAPPA * hist[1, t] * inner
        square = lax.broadcasted_iota(jnp.int32, (slots, slots), 0)
        across = lax.broadcasted_iota(jnp.int32, (slots, slots), 1)
        column = jnp.broadcast_to(info[:, TERMS : TERMS + 1], (slots, slots))
        patch = jnp.sum(jnp.where(square == across, column, 0.0), axis=0, keepdims=True)
        which_patch = lax.broadcasted_iota(jnp.int32, (patches, slots), 0)
        owners = jnp.where(which_patch == patch.astype(jnp.int32), 1.0, 0.0).astype(BF16)
        sums = jnp.dot(
            owners, jnp.concatenate(split(total), axis=1), preferred_element_type=F32
        )
        grad_send[...] = (sums[:, :LANES] + sums[:, LANES:]).reshape(devices, own, LANES)

        @pl.loop(1, devices)
        def _(o):
            grad_copy(lax.rem(me + o, devices)).start()
        grad_recv[me] = grad_send[me]

    row_id = lax.broadcasted_iota(jnp.int32, (cx, LANES), 0)
    lane_id = lax.broadcasted_iota(jnp.int32, (cx, LANES), 1)

    gather(now["a"], "a", 0)
    wait_info()
    gather(now["p"], "p", 0)
    waited = {"ap": False, "s": False, "pp": False}
    gathered = {("a", 0), ("p", 0)}
    sent = False

    for name, step in ORDER:
        field = which[name]
        last = step == STEPS - 1
        ring = buffers[name]
        earlier, current = ring[step % 3], ring[(step + 1) % 3]
        result = outs[name] if last else ring[(step + 2) % 3]

        if name == "p" and step < 2:
            wait_relay(step)
        back = surf[step] if name == "p" else jnp.zeros((slots, LANES), F32)
        for t in range(step + 1):
            back = back + scale[step - t] * hist[field, t]
        if name == "p":
            backs[step] = back
            if last:
                correlate()
        delta = BETA * (back - hist[field, step])
        both = jnp.concatenate(split(delta), axis=0)

        @pl.loop(0, 4)
        def _(part):
            span = pl.ds(pl.multiple_of(part * (cz // 4), cz // 4), cz // 4)
            couple[span] = jnp.dot(
                spread[span].reshape(cz // 4 * blocks * cx, 2 * slots), both,
                preferred_element_type=F32,
            ).reshape(cz // 4, blocks, cx, LANES)

        for need in ((name + "p",) if step == 0 else ()) + ("s",):
            if not waited[need]:
                waited[need] = True
                for copy in loads[need]:
                    copy.wait()
        wait_recv(name, step)
        if step > 0:
            wait_send(name, step - 1, earlier)

        def plane(z, down, up):
            f = [current[z, rb] for rb in range(blocks)]
            right = [pltpu.roll(part, 1, 1) for part in f]
            left = [pltpu.roll(part, LANES - 1, 1) for part in f]
            for rb in range(blocks):
                lo = x_recv[step, field, 0, z, rb : rb + 1, :]
                hi = x_recv[step, field, 1, z, rb : rb + 1, :]
                west = jnp.where(row_id == 0, lo, pltpu.roll(f[rb], 1, 0))
                east = jnp.where(row_id == cx - 1, hi, pltpu.roll(f[rb], cx - 1, 0))
                south = jnp.where(lane_id == 0, right[rb - 1] if rb else 0.0, right[rb])
                north = jnp.where(
                    lane_id == LANES - 1, left[rb + 1] if rb < blocks - 1 else 0.0, left[rb]
                )
                beside = (down[rb] + up[rb]) + (west + east) + (south + north)
                new = (2.0 * f[rb] - earlier[z, rb] + couple[z, rb]) + speed2[z, rb] * (
                    beside - 6.0 * f[rb]
                )
                if last:
                    result[z, :, rb * LANES : (rb + 1) * LANES] = new
                else:
                    result[z, rb] = new
                    x_send[step + 1, field, 0, z, rb : rb + 1, :] = new[0:1]
                    x_send[step + 1, field, 1, z, rb : rb + 1, :] = new[cx - 1 : cx]

        plane(0, z_recv.at[step, field, 0], current.at[1])
        plane(cz - 1, current.at[cz - 2], z_recv.at[step, field, 1])

        @pl.loop(1, cz - 1)
        def _(z):
            plane(z, current.at[z - 1], current.at[z + 1])

        if last:
            wait_send(name, step, current)
        else:
            start_halo(name, step + 1, result)
            gather(result, name, step + 1)

    side = grad_recv.at[pl.ds(0, devices - 1)]
    pltpu.make_async_remote_copy(
        src_ref=side, dst_ref=side, send_sem=grad_ssem, recv_sem=grad_rsem,
        device_id=where_is(lax.rem(me + 1, devices)), device_id_type=MESH,
    ).wait_recv()
    grad_out[...] = jnp.sum(grad_recv[...], axis=0)

    for part, sem, buf in (
        (0, grad_ssem, grad_send.at[pl.ds(0, devices - 1)]),
        (0, info_ssem, info_send.at[pl.ds(0, devices - 1)]),
        (0, relay_ssem.at[0], relay_send.at[pl.ds(0, devices - 1), pl.ds(0, 1)]),
        (1, relay_ssem.at[1], relay_send.at[pl.ds(0, devices - 1), pl.ds(1, TERMS - 1)]),
    ):
        pltpu.make_async_remote_copy(
            src_ref=buf, dst_ref=buf, send_sem=sem, recv_sem=grad_rsem,
            device_id=where_is(lax.rem(me + 1, devices)), device_id_type=MESH,
        ).wait_send()


def body(
    nx, nz, pressure_now, pressure_prev, adjoint_now, adjoint_prev, speed2,
    layer_state, layer_maps, send_rows, slot_patch, patch_material,
):
    slots, depth, width = layer_state.shape
    devices = nx * nz
    patches = patch_material.shape[0]
    mats = layer_maps.shape[0]
    cap = slots // devices
    own = patches // devices
    cz, cx, ny = speed2.shape
    src = send_rows.reshape(-1)
    vmem = pl.BlockSpec(memory_space=pltpu.VMEM)
    smem = pl.BlockSpec(memory_space=pltpu.SMEM)
    hbm = pl.BlockSpec(memory_space=pl.ANY)
    dma = pltpu.SemaphoreType.DMA
    blocks = ny // LANES
    tile = pltpu.VMEM((cz, blocks, cx, LANES), F32)
    rows = pltpu.VMEM((devices, cap, width), F32)
    return pl.pallas_call(
        functools.partial(kernel_body, nx, nz),
        out_shape=(
            jax.ShapeDtypeStruct((cz, cx, ny), F32),
            jax.ShapeDtypeStruct((cz, cx, ny), F32),
            jax.ShapeDtypeStruct((own, width), F32),
        ),
        in_specs=[smem] * 3 + [vmem] * 3 + [hbm] * 6,
        out_specs=(vmem, vmem, vmem),
        scratch_shapes=[
            tile, tile, tile, tile, tile, tile, tile,
            pltpu.VMEM((slots, depth, width), F32),
            pltpu.VMEM((cz, blocks, cx, 2 * slots), BF16),
            tile,
            pltpu.VMEM((2, STEPS, slots, LANES), F32),
            pltpu.VMEM((4 * depth, mats * depth), BF16),
            pltpu.VMEM((TERMS, mats, LANES), F32),
            pltpu.VMEM((mats, 16, LANES), BF16),
            pltpu.VMEM((mats, LANES), F32),
            rows, rows,
            pltpu.VMEM((slots, width), F32),
            pltpu.VMEM((devices, TERMS, cap, width), F32),
            pltpu.VMEM((devices, TERMS, cap, width), F32),
            pltpu.VMEM((TERMS, slots, width), F32),
            pltpu.VMEM((STEPS, slots, width), F32),
            pltpu.VMEM((TERMS, slots, width), F32),
            pltpu.VMEM((devices, own, width), F32),
            pltpu.VMEM((devices, own, width), F32),
            pltpu.VMEM((STEPS, 2, 2, cz, blocks, LANES), F32),
            pltpu.VMEM((STEPS, 2, 2, cz, blocks, LANES), F32),
            pltpu.VMEM((STEPS, 2, 2, blocks, cx, LANES), F32),
            dma((5, blocks)), dma((slots // CHUNK,)),
            dma((STEPS, 2, 4)), dma((STEPS, 2, 4)),
            dma, dma, dma((2,)), dma((2,)), dma, dma,
        ],
        compiler_params=pltpu.CompilerParams(
            collective_id=0, has_side_effects=True, vmem_limit_bytes=56 * 1024 * 1024
        ),
    )(
        slot_patch, patch_material, src, layer_maps, src.reshape(1, slots), src.reshape(slots, 1),
        pressure_now, pressure_prev, adjoint_now, adjoint_prev, speed2, layer_state,
    )


def solution(mesh):
    in_specs = (
        P("gz", "gx", None),
        P("gz", "gx", None),
        P("gz", "gx", None),
        P("gz", "gx", None),
        P("gz", "gx", None),
        P(("gx", "gz"), None, None),
        P(),
        P(("gx", "gz"), None, None),
        P(("gx", "gz")),
        P(),
    )
    out_specs = (P("gz", "gx", None), P("gz", "gx", None), P(("gx", "gz"), None))
    return jax.shard_map(
        functools.partial(body, mesh.shape["gx"], mesh.shape["gz"]),
        mesh=mesh, in_specs=in_specs, out_specs=out_specs, check_vma=False,
    )
```

```python
import functools

import jax
import jax.numpy as jnp
from jax import lax
from jax.experimental import pallas as pl
from jax.experimental.pallas import tpu as pltpu
from jax.sharding import PartitionSpec as P

STEPS = 4
KAPPA = 0.5
BETA = 0.3
TERMS = STEPS + 1
LANES = 128
CHUNK = 16
UNROLL = 8
F32 = jnp.float32
BF16 = jnp.bfloat16
MESH = pl.DeviceIdType.MESH


def split(value):
    high = value.astype(BF16)
    return high, (value - high.astype(F32)).astype(BF16)


def kernel_body(
    nx, nz,
    patch_s, material_s, rows_s, maps,
    p_now_h, p_prev_h, a_now_h, a_prev_h, speed2_h, state_h,
    p_out, a_out, grad_out,
    p_now, p_prev, p_mid, a_now, a_prev, a_mid, speed2, state,
    spread, couple, valid, place, lane_row, hist, weights, chain, table, ctab,
    info_send, info_recv, info, relay_send, relay_recv, surf, backs, scale,
    grad_send, grad_recv, x_send, x_recv, z_recv,
    load_sem, chunk_sem, send_sem, recv_sem,
    info_ssem, info_rsem, relay_ssem, relay_rsem, grad_ssem, grad_rsem,
):
    cz, blocks, cx, _ = speed2.shape
    devices, cap = rows_s.shape
    slots = devices * cap
    mats, depth, _ = maps.shape
    patches = material_s.shape[0]
    own = patches // devices
    chunks = slots // CHUNK
    peers = CHUNK // cap

    gx, gz = lax.axis_index("gx"), lax.axis_index("gz")
    me = gx * nz + gz
    exists = [gx > 0, gx < nx - 1, gz > 0, gz < nz - 1]
    target = [(gx - 1, gz), (gx + 1, gz), (gx, gz - 1), (gx, gz + 1)]

    def where_is(flat):
        return (lax.div(flat, nz), lax.rem(flat, nz))

    first_chunk = lax.div(me * cap, CHUNK)
    loads = {}
    for i, (name, src, dst) in enumerate((
        ("a", a_now_h, a_now), ("p", p_now_h, p_now),
        ("ap", a_prev_h, a_prev), ("s", speed2_h, speed2), ("pp", p_prev_h, p_prev),
    )):
        loads[name] = [
            pltpu.make_async_copy(
                src.at[:, :, pl.ds(rb * LANES, LANES)],
                dst.at[:, rb] if name == "s" else dst.at[pl.ds(1, cz), rb],
                load_sem.at[i, rb],
            )
            for rb in range(blocks)
        ]

    def chunk_copy(j):
        at = lax.rem(first_chunk + j, chunks) * CHUNK
        return pltpu.make_async_copy(
            state_h.at[pl.ds(at, CHUNK)], state.at[pl.ds(at, CHUNK)], chunk_sem.at[j]
        )

    barrier = pltpu.get_barrier_semaphore()

    @pl.loop(1, devices)
    def _(o):
        pl.semaphore_signal(
            barrier, inc=1, device_id=where_is(lax.rem(me + o, devices)), device_id_type=MESH
        )

    for name in ("a", "p"):
        for copy in loads[name]:
            copy.start()

    @pl.loop(0, chunks)
    def _(j):
        chunk_copy(j).start()

    for name in ("ap", "s", "pp"):
        for copy in loads[name]:
            copy.start()

    row8 = lax.broadcasted_iota(jnp.int32, (mats, LANES), 0)
    lane8 = lax.broadcasted_iota(jnp.int32, (mats, LANES), 1)
    halve = jnp.where(lane8 % depth == 0, 1.0 - KAPPA, 1.0)
    for j in range(mats // 2):
        high, low = split(jnp.concatenate([maps[2 * j], maps[2 * j + 1]], axis=1))
        weights[:, j * LANES : (j + 1) * LANES] = jnp.concatenate([high, low, high, low], axis=0)
    v = jnp.concatenate([maps[m, 0:1, :] for m in range(mats)], axis=0)
    v = jnp.concatenate([v, v], axis=1) * halve
    coefs = jnp.zeros((mats, LANES), F32)
    for n in range(TERMS):
        chain[n] = v
        coefs = jnp.where(lane8 == n, v[:, 0:1] * (KAPPA / (1.0 - KAPPA)), coefs)
        if n < TERMS - 1:
            high, low = split(v)
            got = jnp.dot(
                jnp.concatenate([high, low], axis=1), weights[...], preferred_element_type=F32
            )
            total = jnp.zeros((mats, LANES), F32)
            for j in range(mats // 2):
                keep = 2 * j + lane8 // depth == row8
                total = total + jnp.where(keep, got[:, j * LANES : (j + 1) * LANES], 0.0)
            v = (total + pltpu.roll(total, depth, 1)) * halve
    ctab[...] = coefs
    low_half = lax.broadcasted_iota(jnp.int32, (8, LANES), 1) < depth
    for m in range(mats):
        rows = jnp.concatenate(
            [chain[n, m : m + 1, :] for n in range(TERMS)] + [jnp.zeros((8 - TERMS, LANES), F32)],
            axis=0,
        )
        high = rows.astype(BF16)
        low = jnp.where(low_half, rows - high.astype(F32), 0.0).astype(BF16)
        table[m] = jnp.concatenate([high, low], axis=0)

    lane1 = lax.broadcasted_iota(jnp.int32, (1, LANES), 1)
    slot_lane = lax.broadcasted_iota(jnp.int32, (1, slots), 1)
    bit_b, bit_x = blocks.bit_length() - 1, cx.bit_length() - 1

    def index_rows(k, row):
        for c in range(cap):
            raw = rows_s[k, c]
            row = jnp.where(slot_lane == k * cap + c, raw, row)
            r = jnp.maximum(raw, 0)
            z = lax.shift_right_logical(r, bit_b + bit_x)
            x = lax.shift_right_logical(r, bit_b) & (cx - 1)
            place[k * cap + c] = ((z + 1) * blocks + (r & (blocks - 1))) * cx + x
        return row

    lane_row[...] = lax.fori_loop(
        0, devices, index_rows, jnp.full((1, slots), -1, jnp.int32), unroll=4
    )

    @pl.loop(0, devices)
    def _(k):
        for c in range(cap):
            patch = patch_s[k * cap + c]
            coef = ctab[pl.ds(material_s[patch], 1), :]
            ids = jnp.full((1, LANES), patch, jnp.int32).astype(F32)
            info_send[k, c : c + 1, :] = jnp.where(lane1 == TERMS, ids, coef)

    now = {"p": p_now, "a": a_now}
    buffers = {"p": (p_prev, p_now, p_mid), "a": (a_prev, a_now, a_mid)}
    outs = {"p": p_out, "a": a_out}
    which = {"p": 0, "a": 1}

    def halo_copy(name, step, d, source):
        field = which[name]
        if d < 2:
            ref, dst = x_send.at[step, field, d], x_recv.at[step, field, 1 - d]
        else:
            ref = source.at[1 if d == 2 else cz]
            dst = z_recv.at[step, field, 3 - d]
        return pltpu.make_async_remote_copy(
            src_ref=ref, dst_ref=dst,
            send_sem=send_sem.at[step, field, d],
            recv_sem=recv_sem.at[step, field, d ^ 1],
            device_id=target[d], device_id_type=MESH,
        )

    def start_halo(name, step, source):
        for d in range(4):
            @pl.when(exists[d])
            def _(d=d):
                halo_copy(name, step, d, source).start()

    def wait_recv(name, step):
        field = which[name]
        for d in range(4):
            @pl.when(exists[d])
            def _(d=d):
                side = x_recv.at[step, field, d] if d < 2 else z_recv.at[step, field, d - 2]
                pltpu.make_async_remote_copy(
                    src_ref=side, dst_ref=side,
                    send_sem=send_sem.at[step, field, d],
                    recv_sem=recv_sem.at[step, field, d],
                    device_id=target[d], device_id_type=MESH,
                ).wait_recv()

    def wait_send(name, step, source):
        for d in range(4):
            @pl.when(exists[d])
            def _(d=d):
                halo_copy(name, step, d, source).wait_send()

    for d in range(4):
        @pl.when(jnp.logical_not(exists[d]))
        def _(d=d):
            for step in range(STEPS):
                for field in range(2):
                    if d < 2:
                        x_recv[step, field, d] = jnp.zeros((cz, blocks, LANES), F32)
                    else:
                        z_recv[step, field, d - 2] = jnp.zeros((blocks, cx, LANES), F32)

    for name in ("a", "p"):
        for copy in loads[name]:
            copy.wait()

        @pl.loop(0, cz)
        def _(z, name=name):
            for rb in range(blocks):
                x_send[0, which[name], 0, z, rb : rb + 1, :] = now[name][z + 1, rb, 0:1, :]
                x_send[0, which[name], 1, z, rb : rb + 1, :] = now[name][z + 1, rb, cx - 1 : cx, :]

    pl.semaphore_wait(barrier, devices - 1)
    start_halo("a", 0, now["a"])
    start_halo("p", 0, now["p"])

    @pl.loop(1, devices)
    def _(o):
        k = lax.rem(me + o, devices)
        pltpu.make_async_remote_copy(
            src_ref=info_send.at[k], dst_ref=info_recv.at[me],
            send_sem=info_ssem, recv_sem=info_rsem,
            device_id=where_is(k), device_id_type=MESH,
        ).start()

    def relay_copy(k, part):
        rows = pl.ds(0, 1) if part == 0 else pl.ds(1, TERMS - 1)
        return pltpu.make_async_remote_copy(
            src_ref=relay_send.at[k, rows], dst_ref=relay_recv.at[me, rows],
            send_sem=relay_ssem.at[part], recv_sem=relay_rsem.at[part],
            device_id=where_is(k), device_id_type=MESH,
        )

    @pl.loop(0, chunks)
    def _(j):
        chunk = lax.rem(first_chunk + j, chunks)
        chunk_copy(j).wait()
        for pair in range(CHUNK // 2):
            at = chunk * CHUNK + 2 * pair
            mat = [material_s[patch_s[at + i]] for i in range(2)]
            data = jnp.concatenate([state[at], state[at + 1]], axis=1)
            high, low = split(data)
            both = jnp.dot(
                jnp.concatenate([table[mat[0]], table[mat[1]]], axis=0),
                jnp.concatenate([high, low], axis=0), preferred_element_type=F32,
            )
            for i in range(2):
                part = both[16 * i : 16 * i + 16, i * LANES : (i + 1) * LANES]
                got = part[:8] + part[8:]
                slot = 2 * pair + i
                for n in range(TERMS):
                    relay_send[
                        chunk * peers + slot // cap, n, slot % cap : slot % cap + 1, :
                    ] = got[n : n + 1]
        for q in range(peers):
            k = chunk * peers + q
            @pl.when(k != me)
            def _(k=k):
                relay_copy(k, 0).start()
                relay_copy(k, 1).start()

    def gather(source, name, step):
        field = which[name]
        flat = source.reshape((cz + 2) * blocks * cx, LANES)

        @pl.loop(0, slots // 8, unroll=4)
        def _(b):
            base = pl.multiple_of(b * 8, 8)
            picked = [flat[pl.ds(place[base + i], 1), :] for i in range(8)]
            hist[field, step, pl.ds(base, 8), :] = jnp.where(
                valid[pl.ds(base, 8), :] > 0.0, jnp.concatenate(picked, axis=0), 0.0
            )

    def wait_info():
        side = info_recv.at[pl.ds(0, devices - 1)]
        pltpu.make_async_remote_copy(
            src_ref=side, dst_ref=side, send_sem=info_ssem, recv_sem=info_rsem,
            device_id=where_is(lax.rem(me + 1, devices)), device_id_type=MESH,
        ).wait_recv()
        info_recv[me] = info_send[me]
        for k in range(devices):
            info[k * cap : (k + 1) * cap, :] = info_recv[k]
        for n in range(TERMS):
            scale[n] = jnp.broadcast_to(info[:, n : n + 1], (slots, LANES))

    def wait_relay(part):
        rows = pl.ds(0, 1) if part == 0 else pl.ds(1, TERMS - 1)
        side = relay_recv.at[pl.ds(0, devices - 1), rows]
        pltpu.make_async_remote_copy(
            src_ref=side, dst_ref=side, send_sem=relay_ssem.at[part], recv_sem=relay_rsem.at[part],
            device_id=where_is(lax.rem(me + 1, devices)), device_id_type=MESH,
        ).wait_recv()
        for n in ([0] if part == 0 else range(1, TERMS)):
            relay_recv[me, n] = relay_send[me, n]
            for k in range(devices):
                surf[n, k * cap : (k + 1) * cap, :] = relay_recv[k, n]

    def grad_copy(k):
        return pltpu.make_async_remote_copy(
            src_ref=grad_send.at[k], dst_ref=grad_recv.at[me],
            send_sem=grad_ssem, recv_sem=grad_rsem,
            device_id=where_is(k), device_id_type=MESH,
        )

    def back_rows(name, step):
        back = surf[step] if name == "p" else jnp.zeros((slots, LANES), F32)
        for t in range(step + 1):
            back = back + scale[step - t] * hist[which[name], t]
        return back

    def correlate():
        backs[STEPS - 1] = back_rows("p", STEPS - 1)
        total = jnp.zeros((slots, LANES), F32)
        for t in range(STEPS):
            inner = float(STEPS - t) * surf[STEPS - t]
            for q in range(STEPS - t):
                inner = inner + float(STEPS - t - q) * scale[STEPS - t - q] * hist[0, q]
                inner = inner + scale[STEPS - 1 - t - q] * backs[q]
            total = total + KAPPA * hist[1, t] * inner
        column = jnp.broadcast_to(info[:, TERMS : TERMS + 1], (slots, slots))
        patch = jnp.sum(jnp.where(square == across, column, 0.0), axis=0, keepdims=True)
        which_patch = lax.broadcasted_iota(jnp.int32, (patches, slots), 0)
        owners = jnp.where(which_patch == patch.astype(jnp.int32), 1.0, 0.0).astype(BF16)
        sums = jnp.dot(
            owners, jnp.concatenate(split(total), axis=1), preferred_element_type=F32
        )
        grad_send[...] = (sums[:, :LANES] + sums[:, LANES:]).reshape(devices, own, LANES)

        @pl.loop(1, devices)
        def _(o):
            grad_copy(lax.rem(me + o, devices)).start()
        grad_recv[me] = grad_send[me]

    lanes = lane_row[...]
    square = lax.broadcasted_iota(jnp.int32, (slots, slots), 0)
    across = lax.broadcasted_iota(jnp.int32, (slots, slots), 1)
    used = jnp.where(lanes >= 0, 1.0, 0.0)
    column = jnp.sum(jnp.where(square == across, used, 0.0), axis=1, keepdims=True)
    valid[...] = jnp.broadcast_to(column, (slots, LANES))
    xrow = lax.broadcasted_iota(jnp.int32, (cx, slots), 0)

    @pl.loop(0, cz)
    def _(z):
        for rb in range(blocks):
            row = z * (cx * blocks) + xrow * blocks + rb
            hit = jnp.where(row == lanes, 1.0, 0.0).astype(BF16)
            spread[z, rb] = jnp.concatenate([hit, hit], axis=1)

    row_id = lax.broadcasted_iota(jnp.int32, (cx, LANES), 0)
    lane_id = lax.broadcasted_iota(jnp.int32, (cx, LANES), 1)

    gather(now["a"], "a", 0)
    wait_info()
    gather(now["p"], "p", 0)
    waited = {"ap": False, "s": False, "pp": False}
    gathered = {("a", 0), ("p", 0)}
    sent = False

    for step, name in [(step, name) for step in range(STEPS) for name in ("a", "p")]:
        field = which[name]
        last = step == STEPS - 1
        ring = buffers[name]
        earlier, current = ring[step % 3], ring[(step + 1) % 3]
        result = outs[name] if last else ring[(step + 2) % 3]

        if name == "p" and step < 2:
            wait_relay(step)
        if last and name == "a":
            correlate()
        if last and name == "p":
            back = backs[step]
        else:
            back = back_rows(name, step)
        if name == "p":
            backs[step] = back
        delta = BETA * (back - hist[field, step])
        both = jnp.concatenate(split(delta), axis=0)

        @pl.loop(0, 4, unroll=True)
        def _(part):
            span = pl.ds(pl.multiple_of(part * (cz // 4), cz // 4), cz // 4)
            couple[span] = jnp.dot(
                spread[span].reshape(cz // 4 * blocks * cx, 2 * slots), both,
                preferred_element_type=F32,
            ).reshape(cz // 4, blocks, cx, LANES)

        for need in ((name + "p",) if step == 0 else ()) + ("s",):
            if not waited[need]:
                waited[need] = True
                for copy in loads[need]:
                    copy.wait()
        wait_recv(name, step)
        if step > 0:
            wait_send(name, step - 1, earlier)

        current[0] = z_recv[step, field, 0]
        current[cz + 1] = z_recv[step, field, 1]

        @pl.loop(0, cz, unroll=UNROLL)
        def _(z):
            f = [current[z + 1, rb] for rb in range(blocks)]
            right = [pltpu.roll(part, 1, 1) for part in f]
            left = [pltpu.roll(part, LANES - 1, 1) for part in f]
            for rb in range(blocks):
                lo = x_recv[step, field, 0, z, rb : rb + 1, :]
                hi = x_recv[step, field, 1, z, rb : rb + 1, :]
                west = jnp.where(row_id == 0, lo, pltpu.roll(f[rb], 1, 0))
                east = jnp.where(row_id == cx - 1, hi, pltpu.roll(f[rb], cx - 1, 0))
                south = jnp.where(lane_id == 0, right[rb - 1] if rb else 0.0, right[rb])
                north = jnp.where(
                    lane_id == LANES - 1, left[rb + 1] if rb < blocks - 1 else 0.0, left[rb]
                )
                beside = (current[z, rb] + current[z + 2, rb]) + (west + east) + (south + north)
                new = (2.0 * f[rb] - earlier[z + 1, rb] + couple[z, rb]) + speed2[z, rb] * (
                    beside - 6.0 * f[rb]
                )
                if last:
                    result[z, :, rb * LANES : (rb + 1) * LANES] = new
                else:
                    result[z + 1, rb] = new
                    x_send[step + 1, field, 0, z, rb : rb + 1, :] = new[0:1]
                    x_send[step + 1, field, 1, z, rb : rb + 1, :] = new[cx - 1 : cx]

        if last:
            wait_send(name, step, current)
        else:
            start_halo(name, step + 1, result)
            gather(result, name, step + 1)

    side = grad_recv.at[pl.ds(0, devices - 1)]
    pltpu.make_async_remote_copy(
        src_ref=side, dst_ref=side, send_sem=grad_ssem, recv_sem=grad_rsem,
        device_id=where_is(lax.rem(me + 1, devices)), device_id_type=MESH,
    ).wait_recv()
    grad_out[...] = jnp.sum(grad_recv[...], axis=0)

    for part, sem, buf in (
        (0, grad_ssem, grad_send.at[pl.ds(0, devices - 1)]),
        (0, info_ssem, info_send.at[pl.ds(0, devices - 1)]),
        (0, relay_ssem.at[0], relay_send.at[pl.ds(0, devices - 1), pl.ds(0, 1)]),
        (1, relay_ssem.at[1], relay_send.at[pl.ds(0, devices - 1), pl.ds(1, TERMS - 1)]),
    ):
        pltpu.make_async_remote_copy(
            src_ref=buf, dst_ref=buf, send_sem=sem, recv_sem=grad_rsem,
            device_id=where_is(lax.rem(me + 1, devices)), device_id_type=MESH,
        ).wait_send()


def body(
    nx, nz, pressure_now, pressure_prev, adjoint_now, adjoint_prev, speed2,
    layer_state, layer_maps, send_rows, slot_patch, patch_material,
):
    slots, depth, width = layer_state.shape
    devices = nx * nz
    patches = patch_material.shape[0]
    mats = layer_maps.shape[0]
    cap = slots // devices
    own = patches // devices
    cz, cx, ny = speed2.shape
    vmem = pl.BlockSpec(memory_space=pltpu.VMEM)
    smem = pl.BlockSpec(memory_space=pltpu.SMEM)
    hbm = pl.BlockSpec(memory_space=pltpu.HBM)
    dma = pltpu.SemaphoreType.DMA
    blocks = ny // LANES
    tile = pltpu.VMEM((cz, blocks, cx, LANES), F32)
    halo = pltpu.VMEM((cz + 2, blocks, cx, LANES), F32)
    rows = pltpu.VMEM((devices, cap, width), F32)
    return pl.pallas_call(
        functools.partial(kernel_body, nx, nz),
        out_shape=(
            jax.ShapeDtypeStruct((cz, cx, ny), F32),
            jax.ShapeDtypeStruct((cz, cx, ny), F32),
            jax.ShapeDtypeStruct((own, width), F32),
        ),
        in_specs=[smem] * 3 + [vmem] + [hbm] * 6,
        out_specs=(vmem, vmem, vmem),
        scratch_shapes=[
            halo, halo, halo, halo, halo, halo, tile,
            pltpu.VMEM((slots, depth, width), F32),
            pltpu.VMEM((cz, blocks, cx, 2 * slots), BF16),
            tile,
            pltpu.VMEM((slots, LANES), F32),
            pltpu.SMEM((slots,), jnp.int32),
            pltpu.VMEM((1, slots), jnp.int32),
            pltpu.VMEM((2, STEPS, slots, LANES), F32),
            pltpu.VMEM((4 * depth, mats * depth), BF16),
            pltpu.VMEM((TERMS, mats, LANES), F32),
            pltpu.VMEM((mats, 16, LANES), BF16),
            pltpu.VMEM((mats, LANES), F32),
            rows, rows,
            pltpu.VMEM((slots, width), F32),
            pltpu.VMEM((devices, TERMS, cap, width), F32),
            pltpu.VMEM((devices, TERMS, cap, width), F32),
            pltpu.VMEM((TERMS, slots, width), F32),
            pltpu.VMEM((STEPS, slots, width), F32),
            pltpu.VMEM((TERMS, slots, width), F32),
            pltpu.VMEM((devices, own, width), F32),
            pltpu.VMEM((devices, own, width), F32),
            pltpu.VMEM((STEPS, 2, 2, cz, blocks, LANES), F32),
            pltpu.VMEM((STEPS, 2, 2, cz, blocks, LANES), F32),
            pltpu.VMEM((STEPS, 2, 2, blocks, cx, LANES), F32),
            dma((5, blocks)), dma((slots // CHUNK,)),
            dma((STEPS, 2, 4)), dma((STEPS, 2, 4)),
            dma, dma, dma((2,)), dma((2,)), dma, dma,
        ],
        compiler_params=pltpu.CompilerParams(
            collective_id=0, has_side_effects=True, vmem_limit_bytes=51 * 1024 * 1024
        ),
    )(
        slot_patch, patch_material, send_rows.reshape(devices, cap), layer_maps,
        pressure_now, pressure_prev, adjoint_now, adjoint_prev, speed2, layer_state,
    )


def solution(mesh):
    in_specs = (
        P("gz", "gx", None),
        P("gz", "gx", None),
        P("gz", "gx", None),
        P("gz", "gx", None),
        P("gz", "gx", None),
        P(("gx", "gz"), None, None),
        P(),
        P(("gx", "gz"), None, None),
        P(("gx", "gz")),
        P(),
    )
    out_specs = (P("gz", "gx", None), P("gz", "gx", None), P(("gx", "gz"), None))
    return jax.shard_map(
        functools.partial(body, mesh.shape["gx"], mesh.shape["gz"]),
        mesh=mesh, in_specs=in_specs, out_specs=out_specs, check_vma=False,
    )
```

```python
import functools

import jax
import jax.numpy as jnp
from jax import lax
from jax.experimental import pallas as pl
from jax.experimental.pallas import tpu as pltpu
from jax.sharding import PartitionSpec as P

STEPS = 4
KAPPA = 0.5
BETA = 0.3
TERMS = STEPS + 1
LANES = 128
CHUNK = 16
UNROLL = 8
F32 = jnp.float32
BF16 = jnp.bfloat16
MESH = pl.DeviceIdType.MESH


def split(value):
    high = value.astype(BF16)
    return high, (value - high.astype(F32)).astype(BF16)


def kernel_body(
    nx, nz,
    patch_s, material_s, rows_s, maps,
    p_now_h, p_prev_h, a_now_h, a_prev_h, speed2_h, state_h,
    p_out, a_out, grad_out,
    p_now, p_prev, p_mid, a_now, a_prev, a_mid, speed2, state,
    spread, couple, valid, place, lane_row, hist, weights, chain, table, ctab,
    info_send, info_recv, info, relay_send, relay_recv, surf, backs, scale,
    grad_send, grad_recv, x_send, x_recv, z_recv,
    load_sem, chunk_sem, send_sem, recv_sem,
    info_ssem, info_rsem, relay_ssem, relay_rsem, grad_ssem, grad_rsem,
):
    _, blocks, cx, _ = speed2.shape
    cz = p_out.shape[0]
    devices, cap = rows_s.shape
    slots = devices * cap
    plane = blocks * cx
    mats, depth, _ = maps.shape
    patches = material_s.shape[0]
    own = patches // devices
    chunks = slots // CHUNK
    peers = CHUNK // cap

    gx, gz = lax.axis_index("gx"), lax.axis_index("gz")
    me = gx * nz + gz
    exists = [gx > 0, gx < nx - 1, gz > 0, gz < nz - 1]
    target = [(gx - 1, gz), (gx + 1, gz), (gx, gz - 1), (gx, gz + 1)]

    def where_is(flat):
        return (lax.div(flat, nz), lax.rem(flat, nz))

    first_chunk = lax.div(me * cap, CHUNK)
    loads = {}
    for i, (name, src, dst) in enumerate((
        ("a", a_now_h, a_now), ("p", p_now_h, p_now),
        ("ap", a_prev_h, a_prev), ("s", speed2_h, speed2), ("pp", p_prev_h, p_prev),
    )):
        loads[name] = [
            pltpu.make_async_copy(
                src.at[:, :, pl.ds(rb * LANES, LANES)],
                dst.at[pl.ds(0 if name == "s" else 1, cz), rb],
                load_sem.at[i, rb],
            )
            for rb in range(blocks)
        ]

    def chunk_copy(j):
        at = lax.rem(first_chunk + j, chunks) * CHUNK
        return pltpu.make_async_copy(
            state_h.at[pl.ds(at, CHUNK)], state.at[pl.ds(at, CHUNK)], chunk_sem.at[j]
        )

    barrier = pltpu.get_barrier_semaphore()

    @pl.loop(1, devices)
    def _(o):
        pl.semaphore_signal(
            barrier, inc=1, device_id=where_is(lax.rem(me + o, devices)), device_id_type=MESH
        )

    for name in ("a", "p"):
        for copy in loads[name]:
            copy.start()

    @pl.loop(0, chunks)
    def _(j):
        chunk_copy(j).start()

    for name in ("ap", "s", "pp"):
        for copy in loads[name]:
            copy.start()

    row8 = lax.broadcasted_iota(jnp.int32, (mats, LANES), 0)
    lane8 = lax.broadcasted_iota(jnp.int32, (mats, LANES), 1)
    halve = jnp.where(lane8 % depth == 0, 1.0 - KAPPA, 1.0)
    for j in range(mats // 2):
        high, low = split(jnp.concatenate([maps[2 * j], maps[2 * j + 1]], axis=1))
        weights[:, j * LANES : (j + 1) * LANES] = jnp.concatenate([high, low, high, low], axis=0)
    v = jnp.concatenate([maps[m, 0:1, :] for m in range(mats)], axis=0)
    v = jnp.concatenate([v, v], axis=1) * halve
    coefs = jnp.zeros((mats, LANES), F32)
    for n in range(TERMS):
        chain[n] = v
        coefs = jnp.where(lane8 == n, v[:, 0:1] * (KAPPA / (1.0 - KAPPA)), coefs)
        if n < TERMS - 1:
            high, low = split(v)
            got = jnp.dot(
                jnp.concatenate([high, low], axis=1), weights[...], preferred_element_type=F32
            )
            total = jnp.zeros((mats, LANES), F32)
            for j in range(mats // 2):
                keep = 2 * j + lane8 // depth == row8
                total = total + jnp.where(keep, got[:, j * LANES : (j + 1) * LANES], 0.0)
            v = (total + pltpu.roll(total, depth, 1)) * halve
    ctab[...] = coefs
    low_half = lax.broadcasted_iota(jnp.int32, (8, LANES), 1) < depth
    for m in range(mats):
        rows = jnp.concatenate(
            [chain[n, m : m + 1, :] for n in range(TERMS)] + [jnp.zeros((8 - TERMS, LANES), F32)],
            axis=0,
        )
        high = rows.astype(BF16)
        low = jnp.where(low_half, rows - high.astype(F32), 0.0).astype(BF16)
        table[m] = jnp.concatenate([high, low], axis=0)

    lane1 = lax.broadcasted_iota(jnp.int32, (1, LANES), 1)
    slot_lane = lax.broadcasted_iota(jnp.int32, (1, slots), 1)
    bit_b, bit_x = blocks.bit_length() - 1, cx.bit_length() - 1

    def index_rows(k, row):
        for c in range(cap):
            raw = rows_s[k, c]
            row = jnp.where(slot_lane == k * cap + c, raw, row)
            r = jnp.maximum(raw, 0)
            z = lax.shift_right_logical(r, bit_b + bit_x)
            x = lax.shift_right_logical(r, bit_b) & (cx - 1)
            place[k * cap + c] = ((z + 1) * blocks + (r & (blocks - 1))) * cx + x
        return row

    lane_row[...] = lax.fori_loop(
        0, devices, index_rows, jnp.full((1, slots), -1, jnp.int32), unroll=4
    )

    @pl.loop(0, devices)
    def _(k):
        for c in range(cap):
            patch = patch_s[k * cap + c]
            coef = ctab[pl.ds(material_s[patch], 1), :]
            ids = jnp.full((1, LANES), patch, jnp.int32).astype(F32)
            info_send[k, c : c + 1, :] = jnp.where(lane1 == TERMS, ids, coef)

    now = {"p": p_now, "a": a_now}
    buffers = {"p": (p_prev, p_now, p_mid), "a": (a_prev, a_now, a_mid)}
    outs = {"p": p_out, "a": a_out}
    which = {"p": 0, "a": 1}

    def halo_copy(name, step, d, source):
        field = which[name]
        if d < 2:
            ref, dst = x_send.at[step, field, d], x_recv.at[step, field, 1 - d]
        else:
            ref = source.at[1 if d == 2 else cz]
            dst = z_recv.at[step, field, 3 - d]
        return pltpu.make_async_remote_copy(
            src_ref=ref, dst_ref=dst,
            send_sem=send_sem.at[step, field, d],
            recv_sem=recv_sem.at[step, field, d ^ 1],
            device_id=target[d], device_id_type=MESH,
        )

    def start_halo(name, step, source):
        for d in range(4):
            @pl.when(exists[d])
            def _(d=d):
                halo_copy(name, step, d, source).start()

    def wait_recv(name, step):
        field = which[name]
        for d in range(4):
            @pl.when(exists[d])
            def _(d=d):
                side = x_recv.at[step, field, d] if d < 2 else z_recv.at[step, field, d - 2]
                pltpu.make_async_remote_copy(
                    src_ref=side, dst_ref=side,
                    send_sem=send_sem.at[step, field, d],
                    recv_sem=recv_sem.at[step, field, d],
                    device_id=target[d], device_id_type=MESH,
                ).wait_recv()

    def wait_send(name, step, source):
        for d in range(4):
            @pl.when(exists[d])
            def _(d=d):
                halo_copy(name, step, d, source).wait_send()

    for d in range(4):
        @pl.when(jnp.logical_not(exists[d]))
        def _(d=d):
            for step in range(STEPS):
                for field in range(2):
                    if d < 2:
                        x_recv[step, field, d] = jnp.zeros((cz * blocks, LANES), F32)
                    else:
                        z_recv[step, field, d - 2] = jnp.zeros((blocks, cx, LANES), F32)

    for name in ("a", "p"):
        for copy in loads[name]:
            copy.wait()

        flat = now[name].reshape((cz + 2) * plane, LANES)
        for d, x in ((0, 0), (1, cx - 1)):
            for b in range(cz * blocks // 8):
                x_send[0, which[name], d, 8 * b : 8 * b + 8, :] = flat[
                    pl.ds(plane + 8 * b * cx + x, 8, stride=cx), :
                ]
        for ref in buffers[name]:
            ref[0] = jnp.zeros((blocks, cx, LANES), F32)
            ref[cz + 1] = jnp.zeros((blocks, cx, LANES), F32)

    @pl.loop(0, chunks)
    def _(j):
        chunk = lax.rem(first_chunk + j, chunks)
        chunk_copy(j).wait()
        for pair in range(CHUNK // 2):
            at = chunk * CHUNK + 2 * pair
            mat = [material_s[patch_s[at + i]] for i in range(2)]
            data = jnp.concatenate([state[at], state[at + 1]], axis=1)
            high, low = split(data)
            both = jnp.dot(
                jnp.concatenate([table[mat[0]], table[mat[1]]], axis=0),
                jnp.concatenate([high, low], axis=0), preferred_element_type=F32,
            )
            for i in range(2):
                part = both[16 * i : 16 * i + 16, i * LANES : (i + 1) * LANES]
                got = part[:8] + part[8:]
                slot = 2 * pair + i
                for n in range(TERMS):
                    relay_send[
                        chunk * peers + slot // cap, n, slot % cap : slot % cap + 1, :
                    ] = got[n : n + 1]

    pl.semaphore_wait(barrier, devices - 1)
    start_halo("a", 0, now["a"])
    start_halo("p", 0, now["p"])

    @pl.loop(1, devices)
    def _(o):
        k = lax.rem(me + o, devices)
        pltpu.make_async_remote_copy(
            src_ref=info_send.at[k], dst_ref=info_recv.at[me],
            send_sem=info_ssem, recv_sem=info_rsem,
            device_id=where_is(k), device_id_type=MESH,
        ).start()

    def relay_copy(k, part):
        rows = pl.ds(part, 1) if part < 2 else pl.ds(2, TERMS - 2)
        return pltpu.make_async_remote_copy(
            src_ref=relay_send.at[k, rows], dst_ref=relay_recv.at[me, rows],
            send_sem=relay_ssem.at[part], recv_sem=relay_rsem.at[part],
            device_id=where_is(k), device_id_type=MESH,
        )

    for part in range(3):
        @pl.loop(1, devices)
        def _(o, part=part):
            relay_copy(lax.rem(me + o, devices), part).start()

    def gather(source, name, step):
        field = which[name]
        flat = source.reshape((cz + 2) * blocks * cx, LANES)

        @pl.loop(0, slots // 8, unroll=4)
        def _(b):
            base = pl.multiple_of(b * 8, 8)
            picked = [flat[pl.ds(place[base + i], 1), :] for i in range(8)]
            hist[field, step, pl.ds(base, 8), :] = jnp.where(
                valid[pl.ds(base, 8), :] > 0.0, jnp.concatenate(picked, axis=0), 0.0
            )

    def wait_info():
        side = info_recv.at[pl.ds(0, devices - 1)]
        pltpu.make_async_remote_copy(
            src_ref=side, dst_ref=side, send_sem=info_ssem, recv_sem=info_rsem,
            device_id=where_is(lax.rem(me + 1, devices)), device_id_type=MESH,
        ).wait_recv()
        info_recv[me] = info_send[me]
        for k in range(devices):
            info[k * cap : (k + 1) * cap, :] = info_recv[k]
        for n in range(TERMS):
            scale[n] = jnp.broadcast_to(info[:, n : n + 1], (slots, LANES))

    def wait_relay(part):
        rows = pl.ds(part, 1) if part < 2 else pl.ds(2, TERMS - 2)
        side = relay_recv.at[pl.ds(0, devices - 1), rows]
        pltpu.make_async_remote_copy(
            src_ref=side, dst_ref=side, send_sem=relay_ssem.at[part], recv_sem=relay_rsem.at[part],
            device_id=where_is(lax.rem(me + 1, devices)), device_id_type=MESH,
        ).wait_recv()
        for n in ([part] if part < 2 else range(2, TERMS)):
            relay_recv[me, n] = relay_send[me, n]
            for k in range(devices):
                surf[n, k * cap : (k + 1) * cap, :] = relay_recv[k, n]

    def grad_copy(k):
        return pltpu.make_async_remote_copy(
            src_ref=grad_send.at[k], dst_ref=grad_recv.at[me],
            send_sem=grad_ssem, recv_sem=grad_rsem,
            device_id=where_is(k), device_id_type=MESH,
        )

    def back_rows(name, step):
        back = surf[step] if name == "p" else jnp.zeros((slots, LANES), F32)
        for t in range(step + 1):
            back = back + scale[step - t] * hist[which[name], t]
        return back

    def correlate():
        backs[STEPS - 1] = back_rows("p", STEPS - 1)
        total = jnp.zeros((slots, LANES), F32)
        for t in range(STEPS):
            inner = float(STEPS - t) * surf[STEPS - t]
            for q in range(STEPS - t):
                inner = inner + float(STEPS - t - q) * scale[STEPS - t - q] * hist[0, q]
                inner = inner + scale[STEPS - 1 - t - q] * backs[q]
            total = total + KAPPA * hist[1, t] * inner
        column = jnp.broadcast_to(info[:, TERMS : TERMS + 1], (slots, slots))
        patch = jnp.sum(jnp.where(square == across, column, 0.0), axis=0, keepdims=True)
        which_patch = lax.broadcasted_iota(jnp.int32, (patches, slots), 0)
        owners = jnp.where(which_patch == patch.astype(jnp.int32), 1.0, 0.0).astype(BF16)
        sums = jnp.dot(
            owners, jnp.concatenate(split(total), axis=1), preferred_element_type=F32
        )
        grad_send[...] = (sums[:, :LANES] + sums[:, LANES:]).reshape(devices, own, LANES)

        @pl.loop(1, devices)
        def _(o):
            grad_copy(lax.rem(me + o, devices)).start()
        grad_recv[me] = grad_send[me]

    lanes = lane_row[...]
    square = lax.broadcasted_iota(jnp.int32, (slots, slots), 0)
    across = lax.broadcasted_iota(jnp.int32, (slots, slots), 1)
    used = jnp.where(lanes >= 0, 1.0, 0.0)
    column = jnp.sum(jnp.where(square == across, used, 0.0), axis=1, keepdims=True)
    valid[...] = jnp.broadcast_to(column, (slots, LANES))
    xrow = lax.broadcasted_iota(jnp.int32, (cx, slots), 0)

    @pl.loop(0, cz)
    def _(z):
        for rb in range(blocks):
            row = z * (cx * blocks) + xrow * blocks + rb
            hit = jnp.where(row == lanes, 1.0, 0.0).astype(BF16)
            spread[z, rb] = jnp.concatenate([hit, hit], axis=1)

    row_id = lax.broadcasted_iota(jnp.int32, (cx, LANES), 0)
    lane_id = lax.broadcasted_iota(jnp.int32, (cx, LANES), 1)

    waited = set()

    def need(*names):
        for item in names:
            if item not in waited:
                waited.add(item)
                for copy in loads[item]:
                    copy.wait()

    def fields(name, step):
        ring = buffers[name]
        return ring[step % 3], ring[(step + 1) % 3], ring[(step + 2) % 3]

    def around(f, rb, right, left, lo, hi):
        west = jnp.where(row_id == 0, lo, pltpu.roll(f[rb], 1, 0))
        east = jnp.where(row_id == cx - 1, hi, pltpu.roll(f[rb], cx - 1, 0))
        south = jnp.where(lane_id == 0, right[rb - 1] if rb else 0.0, right[rb])
        north = jnp.where(lane_id == LANES - 1, left[rb + 1] if rb < blocks - 1 else 0.0, left[rb])
        return (west + east) + (south + north)

    def stencil(name, step):
        earlier, current, result = fields(name, step)
        last = step == STEPS - 1

        @pl.loop(0, cz, unroll=UNROLL)
        def _(z):
            f = [current[z + 1, rb] for rb in range(blocks)]
            right = [pltpu.roll(part, 1, 1) for part in f]
            left = [pltpu.roll(part, LANES - 1, 1) for part in f]
            for rb in range(blocks):
                lo, hi = 0.0, 0.0
                if last:
                    lo = x_recv[step, which[name], 0, pl.ds(z * blocks + rb, 1), :]
                    hi = x_recv[step, which[name], 1, pl.ds(z * blocks + rb, 1), :]
                beside = (current[z, rb] + current[z + 2, rb]) + around(f, rb, right, left, lo, hi)
                new = (2.0 * f[rb] - earlier[z + 1, rb]) + speed2[z, rb] * (beside - 6.0 * f[rb])
                if last:
                    outs[name][z, :, rb * LANES : (rb + 1) * LANES] = new + couple[z, rb]
                else:
                    result[z + 1, rb] = new

    def couplings(name, step):
        if step == STEPS - 1 and name == "p":
            back = backs[step]
        else:
            back = back_rows(name, step)
        if name == "p":
            backs[step] = back
        delta = BETA * (back - hist[which[name], step])
        both = jnp.concatenate(split(delta), axis=0)
        result = fields(name, step)[2]
        size = cz // 4
        for part in range(4):
            at = part * size
            extra = jnp.dot(
                spread[at : at + size].reshape(size * plane, 2 * slots), both,
                preferred_element_type=F32,
            ).reshape(size, blocks, cx, LANES)
            if step == STEPS - 1:
                couple[at : at + size] = extra
            else:
                result[at + 1 : at + 1 + size] = result[at + 1 : at + 1 + size] + extra

    def finish(name, step):
        field = which[name]
        earlier, current, result = fields(name, step)
        wait_recv(name, step)
        if step > 0:
            wait_send(name, step - 1, earlier)
        result[1] = result[1] + speed2[0] * z_recv[step, field, 0]
        result[cz] = result[cz] + speed2[cz - 1] * z_recv[step, field, 1]
        flat = result.reshape((cz + 2) * plane, LANES)
        gain = speed2.reshape((cz + 1) * plane, LANES)
        for d, x in ((0, 0), (1, cx - 1)):
            for b in range(cz * blocks // 8):
                at = 8 * b * cx + x
                new = flat[pl.ds(plane + at, 8, stride=cx), :] + (
                    gain[pl.ds(at, 8, stride=cx), :]
                    * x_recv[step, field, d, 8 * b : 8 * b + 8, :]
                )
                flat[pl.ds(plane + at, 8, stride=cx), :] = new
                x_send[step + 1, field, d, 8 * b : 8 * b + 8, :] = new
        start_halo(name, step + 1, result)
        gather(result, name, step + 1)

    gather(now["a"], "a", 0)
    gather(now["p"], "p", 0)
    for step in range(STEPS - 1):
        need("ap", "s")
        stencil("a", step)
        need("pp")
        stencil("p", step)
        if step == 0:
            wait_info()
        couplings("a", step)
        finish("a", step)
        wait_relay(step)
        couplings("p", step)
        finish("p", step)
    correlate()
    step = STEPS - 1
    for name in ("a", "p"):
        couplings(name, step)
        earlier, current, result = fields(name, step)
        wait_recv(name, step)
        wait_send(name, step - 1, earlier)
        current[0] = z_recv[step, which[name], 0]
        current[cz + 1] = z_recv[step, which[name], 1]
        stencil(name, step)
    for name in ("a", "p"):
        wait_send(name, step, fields(name, step)[1])

    side = grad_recv.at[pl.ds(0, devices - 1)]
    pltpu.make_async_remote_copy(
        src_ref=side, dst_ref=side, send_sem=grad_ssem, recv_sem=grad_rsem,
        device_id=where_is(lax.rem(me + 1, devices)), device_id_type=MESH,
    ).wait_recv()
    grad_out[...] = jnp.sum(grad_recv[...], axis=0)

    for part, sem, buf in (
        (0, grad_ssem, grad_send.at[pl.ds(0, devices - 1)]),
        (0, info_ssem, info_send.at[pl.ds(0, devices - 1)]),
        (0, relay_ssem.at[0], relay_send.at[pl.ds(0, devices - 1), pl.ds(0, 1)]),
        (1, relay_ssem.at[1], relay_send.at[pl.ds(0, devices - 1), pl.ds(1, 1)]),
        (2, relay_ssem.at[2], relay_send.at[pl.ds(0, devices - 1), pl.ds(2, TERMS - 2)]),
    ):
        pltpu.make_async_remote_copy(
            src_ref=buf, dst_ref=buf, send_sem=sem, recv_sem=grad_rsem,
            device_id=where_is(lax.rem(me + 1, devices)), device_id_type=MESH,
        ).wait_send()


def body(
    nx, nz, pressure_now, pressure_prev, adjoint_now, adjoint_prev, speed2,
    layer_state, layer_maps, send_rows, slot_patch, patch_material,
):
    slots, depth, width = layer_state.shape
    devices = nx * nz
    patches = patch_material.shape[0]
    mats = layer_maps.shape[0]
    cap = slots // devices
    own = patches // devices
    cz, cx, ny = speed2.shape
    vmem = pl.BlockSpec(memory_space=pltpu.VMEM)
    smem = pl.BlockSpec(memory_space=pltpu.SMEM)
    hbm = pl.BlockSpec(memory_space=pltpu.HBM)
    dma = pltpu.SemaphoreType.DMA
    blocks = ny // LANES
    tile = pltpu.VMEM((cz, blocks, cx, LANES), F32)
    gain = pltpu.VMEM((cz + 1, blocks, cx, LANES), F32)
    halo = pltpu.VMEM((cz + 2, blocks, cx, LANES), F32)
    rows = pltpu.VMEM((devices, cap, width), F32)
    return pl.pallas_call(
        functools.partial(kernel_body, nx, nz),
        out_shape=(
            jax.ShapeDtypeStruct((cz, cx, ny), F32),
            jax.ShapeDtypeStruct((cz, cx, ny), F32),
            jax.ShapeDtypeStruct((own, width), F32),
        ),
        in_specs=[smem] * 3 + [vmem] + [hbm] * 6,
        out_specs=(vmem, vmem, vmem),
        scratch_shapes=[
            halo, halo, halo, halo, halo, halo, gain,
            pltpu.VMEM((slots, depth, width), F32),
            pltpu.VMEM((cz, blocks, cx, 2 * slots), BF16),
            tile,
            pltpu.VMEM((slots, LANES), F32),
            pltpu.SMEM((slots,), jnp.int32),
            pltpu.VMEM((1, slots), jnp.int32),
            pltpu.VMEM((2, STEPS, slots, LANES), F32),
            pltpu.VMEM((4 * depth, mats * depth), BF16),
            pltpu.VMEM((TERMS, mats, LANES), F32),
            pltpu.VMEM((mats, 16, LANES), BF16),
            pltpu.VMEM((mats, LANES), F32),
            rows, rows,
            pltpu.VMEM((slots, width), F32),
            pltpu.VMEM((devices, TERMS, cap, width), F32),
            pltpu.VMEM((devices, TERMS, cap, width), F32),
            pltpu.VMEM((TERMS, slots, width), F32),
            pltpu.VMEM((STEPS, slots, width), F32),
            pltpu.VMEM((TERMS, slots, width), F32),
            pltpu.VMEM((devices, own, width), F32),
            pltpu.VMEM((devices, own, width), F32),
            pltpu.VMEM((STEPS, 2, 2, cz * blocks, LANES), F32),
            pltpu.VMEM((STEPS, 2, 2, cz * blocks, LANES), F32),
            pltpu.VMEM((STEPS, 2, 2, blocks, cx, LANES), F32),
            dma((5, blocks)), dma((slots // CHUNK,)),
            dma((STEPS, 2, 4)), dma((STEPS, 2, 4)),
            dma, dma, dma((3,)), dma((3,)), dma, dma,
        ],
        compiler_params=pltpu.CompilerParams(
            collective_id=0, has_side_effects=True, vmem_limit_bytes=51 * 1024 * 1024
        ),
    )(
        slot_patch, patch_material, send_rows.reshape(devices, cap), layer_maps,
        pressure_now, pressure_prev, adjoint_now, adjoint_prev, speed2, layer_state,
    )


def solution(mesh):
    in_specs = (
        P("gz", "gx", None),
        P("gz", "gx", None),
        P("gz", "gx", None),
        P("gz", "gx", None),
        P("gz", "gx", None),
        P(("gx", "gz"), None, None),
        P(),
        P(("gx", "gz"), None, None),
        P(("gx", "gz")),
        P(),
    )
    out_specs = (P("gz", "gx", None), P("gz", "gx", None), P(("gx", "gz"), None))
    return jax.shard_map(
        functools.partial(body, mesh.shape["gx"], mesh.shape["gz"]),
        mesh=mesh, in_specs=in_specs, out_specs=out_specs, check_vma=False,
    )
```
